256 devices in a mesh: seq: 32 (over y, z), dp: 8 (over x, core).
Axes of the slice: x: 4, y: 4, z: 8, core: 2. Of those that a mesh axis runs over, the one named last changes fastest.
Arguments:
- frames: bfloat16 [32, 4096, 384], P('dp', 'seq'), may hold values from -48 to 48
- w_query: bfloat16 [384, 384], replicated, may hold values from -0.3125 to 0.3125
- w_key: bfloat16 [384, 384], replicated, may hold values from -0.3125 to 0.3125
- w_value: bfloat16 [384, 384], replicated, may hold values from -0.3125 to 0.3125
- w_out: bfloat16 [384, 384], replicated, may hold values from -0.3125 to 0.3125
- valid_counts: int32 [32, 128], P('dp', 'seq'), may hold values from 1 to 32
- out_grad: bfloat16 [32, 4096, 384], P('dp', 'seq'), may hold values from -6 to 6
Outputs:
- attended: bfloat16 [32, 4096, 384], P('dp', 'seq')
- frame_grads: bfloat16 [32, 4096, 384], P('dp', 'seq')
- weight_grads: float32 [4, 384, 384], replicated
The draws below stay inside these ranges and needn't reach their ends.
Inputs may be any that keep to these rules, and one draw needn't show every extreme that they name: `valid_counts`: valid frames of each span, counted from the span's start.
All inputs are finite; a program needn't handle non-finite values.
Results may differ from the reference program's by a relative error of at most 0.013.
The reference program's roundings to bfloat16 on the way (of `probs_b`, `context`, `d_context`, `d_scores` and `d_query`) count: a program that leaves them out, or rounds other values in their place, can miss the bound.
Values may be sent and summed in bfloat16 or wider, within the bound.
No kernel may reach another device: no remote copies, remote signals or barrier semaphores. Data moves between devices by JAX's collectives and lax.ppermute only.
A program may use at most 64 MiB of HBM per device.

```python
import jax
import jax.numpy as jnp
from jax import lax

D = 384
HEADS = 4
CH = 32
CTX = 128
UTT = 32
FRAMES = 4096
NCHUNK = 128


def draw_frames(key, part):
    base = jnp.clip(jax.random.normal(key, (UTT, FRAMES, D), jnp.float32), -4.0, 4.0)
    return base.astype(jnp.bfloat16)


def plant(array, own_key, low, top_value):
    index_at = [jax.random.randint(jax.random.fold_in(own_key, axis), (), 0, length) for axis, length in enumerate(array.shape)]
    widest = array.shape.index(max(array.shape))
    beside = index_at[:widest] + [(index_at[widest] + 1) % array.shape[widest]] + index_at[widest + 1:]
    return array.at[tuple(index_at)].set(low).at[tuple(beside)].set(top_value)


def shard_levels(key, dims, shards, low, high):
    level = 1.0
    for axis_at, blocks in shards:
        steps = jax.random.uniform(jax.random.fold_in(jax.random.fold_in(key, 6), axis_at), (blocks,), jnp.float32, low / len(shards), high / len(shards))
        level = level * jnp.repeat(jnp.exp(steps), dims[axis_at] // blocks).reshape((-1,) + (1,) * (len(dims) - 1 - axis_at))
    return level


def centred(rng, shape, scale, reach, pieces=(), kind=jnp.bfloat16):
    entries = jax.random.normal(rng, shape, jnp.float32) * scale
    if len(pieces) > 0:
        entries = shard_levels(rng, shape, pieces, -0.22, 0.18) * entries
    return jnp.clip(entries, min=-reach, max=reach).astype(kind)


def setup_inputs(seed: int = 0) -> dict:
    key_of = jax.random.split(jax.random.key(seed), 8)
    frames = draw_frames(jax.random.fold_in(key_of[7], 71), 0)
    w_query = centred(key_of[1], (D, D), D ** -0.5, 0.3125)
    w_key = centred(key_of[2], (D, D), D ** -0.5, 0.3125)
    w_value = centred(key_of[3], (D, D), D ** -0.5, 0.3125)
    w_out = centred(key_of[4], (D, D), D ** -0.5, 0.3125)
    valid_counts = plant(jax.random.randint(key_of[5], (UTT, NCHUNK), 1, CH + 1), jax.random.fold_in(key_of[5], 1), 1, CH).astype(jnp.int32)
    out_grad = centred(key_of[6], (UTT, FRAMES, D), 1.0, 6.0, ((0, 8), (1, 32)))
    return dict(frames=frames, w_query=w_query, w_key=w_key, w_value=w_value, w_out=w_out, valid_counts=valid_counts, out_grad=out_grad)


def windows(padded, nch, wide, ch):
    blocks = padded.reshape((nch + wide - 1, ch) + padded.shape[1:])
    return jnp.concatenate([blocks[i:i + nch] for i in range(wide)], 1)


def unwindow(win, nch, wide, ch):
    rest = win.shape[2:]
    total = jnp.zeros((nch + wide - 1, ch) + rest, win.dtype)
    for i in range(wide):
        total = total.at[i:i + nch].add(win[:, i * ch:(i + 1) * ch])
    return total.reshape(((nch + wide - 1) * ch,) + rest)


def project(data, weight):
    return jnp.dot(data, weight, preferred_element_type=jnp.float32).astype(jnp.bfloat16)


def backdot(data, weight):
    return lax.dot_general(data, weight, (((1,), (1,)), ((), ())), preferred_element_type=jnp.float32)


def coldot(left, right):
    return lax.dot_general(left, right, (((0,), (0,)), ((), ())), preferred_element_type=jnp.float32)


def one_utterance(x, counts, grad, w_query, w_key, w_value, w_out):
    nch = FRAMES // CH
    wide = CTX // CH + 1
    size = D // HEADS
    scale = size ** -0.5
    query = project(x, w_query)
    keys = project(x, w_key)
    values = project(x, w_value)
    zero_rows = jnp.zeros((CTX, D), jnp.bfloat16)
    key_pad = jnp.concatenate([zero_rows, keys], 0)
    value_pad = jnp.concatenate([zero_rows, values], 0)
    count_pad = jnp.concatenate([jnp.zeros((CTX // CH,), jnp.int32), counts.astype(jnp.int32)], 0)
    slots = lax.broadcasted_iota(jnp.int32, (1, CH), 1)
    ok_pad = (slots < count_pad[:, None]).reshape(-1)
    qc = query.reshape(nch, CH, HEADS, size).astype(jnp.float32)
    kw = windows(key_pad, nch, wide, CH).reshape(nch, wide * CH, HEADS, size).astype(jnp.float32)
    vw = windows(value_pad, nch, wide, CH).reshape(nch, wide * CH, HEADS, size).astype(jnp.float32)
    okw = windows(ok_pad, nch, wide, CH)
    scores = jnp.einsum('cqhe,ckhe->chqk', qc, kw) * scale
    scores = jnp.where(okw[:, None, None, :], scores, jnp.float32(-1e30))
    top = jnp.max(scores, -1, keepdims=True)
    expo = jnp.exp(scores - top)
    probs = expo / jnp.sum(expo, -1, keepdims=True)
    probs_b = probs.astype(jnp.bfloat16)
    context = jnp.einsum('chqk,ckhe->cqhe', probs_b.astype(jnp.float32), vw).astype(jnp.bfloat16).reshape(FRAMES, D)
    attended = project(context, w_out)
    d_context = backdot(grad, w_out).astype(jnp.bfloat16)
    dc = d_context.reshape(nch, CH, HEADS, size).astype(jnp.float32)
    d_probs = jnp.einsum('cqhe,ckhe->chqk', dc, vw)
    delta = jnp.sum(probs * d_probs, -1, keepdims=True)
    d_scores = (probs * (d_probs - delta) * scale).astype(jnp.bfloat16).astype(jnp.float32)
    d_query = jnp.einsum('chqk,ckhe->cqhe', d_scores, kw).astype(jnp.bfloat16).reshape(FRAMES, D)
    d_kw = jnp.einsum('chqk,cqhe->ckhe', d_scores, qc).reshape(nch, wide * CH, D)
    d_vw = jnp.einsum('chqk,cqhe->ckhe', probs_b.astype(jnp.float32), dc).reshape(nch, wide * CH, D)
    d_key = unwindow(d_kw, nch, wide, CH)[CTX:].astype(jnp.bfloat16)
    d_value = unwindow(d_vw, nch, wide, CH)[CTX:].astype(jnp.bfloat16)
    frame_grad = (backdot(d_query, w_query) + backdot(d_key, w_key) + backdot(d_value, w_value)).astype(jnp.bfloat16)
    grads = jnp.stack([coldot(x, d_query), coldot(x, d_key), coldot(x, d_value), coldot(context, grad)])
    return attended, frame_grad, grads


def reference(frames, w_query, w_key, w_value, w_out, valid_counts, out_grad):
    def step(total, item):
        x, counts, grad = item
        attended, frame_grad, grads = one_utterance(x, counts, grad, w_query, w_key, w_value, w_out)
        return total + grads, (attended, frame_grad)

    start = jnp.zeros((4, D, D), jnp.float32)
    total, outs = lax.scan(step, start, (frames, valid_counts, out_grad))
    return outs[0], outs[1], total
```

```python
import jax
import jax.numpy as jnp
from jax import lax
from jax.experimental import pallas as pl
from jax.experimental.pallas import tpu as pltpu
from jax.sharding import PartitionSpec as P

HEADS = 4
CH = 32
CTX = 128
LENGTH_Z = 8
CORES = 2
EVERY = ("seq", "dp")
BF16 = jnp.bfloat16
F32 = jnp.float32


def shifted(value, axis, by):
    length = lax.axis_size(axis)
    pairs = [(i, i + by) for i in range(length) if 0 <= i + by < length]
    return lax.ppermute(value, axis, pairs)


def plain(left, right):
    return jnp.dot(left, right, preferred_element_type=F32)


def rows_dot(left, right):
    return lax.dot_general(left, right, (((1,), (1,)), ((), ())), preferred_element_type=F32)


def cols_dot(left, right):
    return lax.dot_general(left, right, (((0,), (0,)), ((), ())), preferred_element_type=F32)


def attention_kernel(
    own_counts, prev_counts, core_ref, x_ref, xp_ref, g_ref, wq_ref, wk_ref, wv_ref, wo_ref,
    att_ref, fg_ref, fgp_ref, keep_ref, send_ref,
    q_s, k_s, v_s, dc_s, ctx_s, dq_s, dk_s, dv_s,
):
    batch, local, width = x_ref.shape
    size = width // HEADS
    scale = size ** (-0.5)
    keys = CTX + local
    many = HEADS * local
    rows = batch * local

    x = x_ref[...].reshape(rows, width)
    xp = xp_ref[...].reshape(rows, width)
    g = g_ref[...].reshape(rows, width)

    def spread(value):
        return value.astype(BF16).reshape(batch, local, width)

    q_s[...] = spread(plain(x, wq_ref[...]))
    dc_s[...] = spread(rows_dot(g, wo_ref[...]))
    k_s[:, CTX:, :] = spread(plain(x, wk_ref[...]))
    v_s[:, CTX:, :] = spread(plain(x, wv_ref[...]))
    k_s[:, :CTX, :] = spread(plain(xp, wk_ref[...]))
    v_s[:, :CTX, :] = spread(plain(xp, wv_ref[...]))

    head_of = lax.broadcasted_iota(jnp.int32, (local, width), 1) // size
    lane_span = (lax.broadcasted_iota(jnp.int32, (CH, many), 1) % local) // CH
    slot = lax.broadcasted_iota(jnp.int32, (CH, many), 0)

    def by_head(value):
        zero = jnp.zeros_like(value)
        return jnp.concatenate([jnp.where(head_of == h, value, zero) for h in range(HEADS)], 0)

    def own_head(wide):
        out = wide[:local]
        for h in range(1, HEADS):
            out = jnp.where(head_of == h, wide[h * local : (h + 1) * local], out)
        return out

    def one(u, carry):
        k = k_s[u]
        v = v_s[u]
        qm = by_head(q_s[u])
        dcm = by_head(dc_s[u])
        scores = rows_dot(k, qm)
        parts = []
        for s in range(keys // CH):
            count = prev_counts[u, s] if s < CTX // CH else own_counts[u, s - CTX // CH]
            behind = s - lane_span
            seen = (slot < count) & (behind >= 0) & (behind <= CTX // CH)
            parts.append(jnp.where(seen, scores[s * CH : (s + 1) * CH] * scale, F32(-1e30)))
        scores = jnp.concatenate(parts, 0)
        top = jnp.max(scores, 0, keepdims=True)
        expo = jnp.exp(scores - top)
        probs = expo * (1.0 / jnp.sum(expo, 0, keepdims=True))
        probs_b = probs.astype(BF16)
        ctx_s[u] = own_head(cols_dot(probs_b, v)).astype(BF16)
        d_probs = rows_dot(v, dcm)
        delta = jnp.sum(probs * d_probs, 0, keepdims=True)
        d_scores = (probs * (d_probs - delta) * scale).astype(BF16)
        dq_s[u] = own_head(cols_dot(d_scores, k)).astype(BF16)
        dk_s[u] = plain(d_scores, qm).astype(BF16)
        dv_s[u] = plain(probs_b, dcm).astype(BF16)
        return carry

    lax.fori_loop(0, batch, one, 0)

    ctx = ctx_s[...].reshape(rows, width)
    dq = dq_s[...].reshape(rows, width)
    dk = dk_s[:, CTX:, :].reshape(rows, width)
    dv = dv_s[:, CTX:, :].reshape(rows, width)
    dkp = dk_s[:, :CTX, :].reshape(rows, width)
    dvp = dv_s[:, :CTX, :].reshape(rows, width)

    att_ref[...] = spread(plain(ctx, wo_ref[...]))
    fgp_ref[...] = spread(rows_dot(dkp, wk_ref[...]) + rows_dot(dvp, wv_ref[...]))
    total = rows_dot(dq, wq_ref[...]) + rows_dot(dk, wk_ref[...]) + rows_dot(dv, wv_ref[...])
    fg_ref[...] = total.reshape(batch, local, width)
    grads = [
        cols_dot(x, dq),
        cols_dot(x, dk) + cols_dot(xp, dkp),
        cols_dot(x, dv) + cols_dot(xp, dvp),
        cols_dot(ctx, g),
    ]
    core = core_ref[0]

    @pl.when(core == 0)
    def _():
        for i in range(2):
            keep_ref[i] = grads[i]
            send_ref[i] = grads[2 + i]

    @pl.when(core != 0)
    def _():
        for i in range(2):
            keep_ref[i] = grads[2 + i]
            send_ref[i] = grads[i]


def attention(own_counts, prev_counts, core, x, xp, g, w_query, w_key, w_value, w_out):
    batch, local, width = x.shape
    smem = pl.BlockSpec(memory_space=pltpu.SMEM)
    vmem = pl.BlockSpec(memory_space=pltpu.VMEM)
    short = pltpu.VMEM((batch, local, width), BF16)
    long = pltpu.VMEM((batch, CTX + local, width), BF16)
    return pl.pallas_call(
        attention_kernel,
        out_shape=[
            jax.ShapeDtypeStruct((batch, local, width), BF16),
            jax.ShapeDtypeStruct((batch, local, width), F32),
            jax.ShapeDtypeStruct((batch, local, width), BF16),
            jax.ShapeDtypeStruct((2, width, width), F32),
            jax.ShapeDtypeStruct((2, width, width), F32),
        ],
        in_specs=[smem] * 3 + [vmem] * 7,
        out_specs=[vmem] * 5,
        scratch_shapes=[short, long, long, short, short, short, long, long],
        name="attention",
    )(own_counts, prev_counts, core, x, xp, g, w_query, w_key, w_value, w_out)


def groups():
    seq, dp = lax.axis_size("seq"), lax.axis_size("dp")
    z, c = min(LENGTH_Z, seq // 2), CORES
    y, x = seq // z, dp // c

    def at(iy, iz, ix, ic):
        return (iy * z + iz) * dp + ix * c + ic

    plane = [
        [at(iy, iz, ix, ic) for iy in range(y) for ix in range(x)] for iz in range(z) for ic in range(c)
    ]
    column = [
        [at(iy, iz, ix, ic) for iz in range(z)] for iy in range(y) for ix in range(x) for ic in range(c)
    ]
    return plane, column


def partner(value):
    pairs = [(i, i ^ 1) for i in range(lax.axis_size("dp"))]
    return lax.ppermute(value, "dp", pairs)


def exchange(value, members):
    return lax.all_to_all(value, EVERY, 0, 0, axis_index_groups=members)


def to_all(value, members):
    return exchange(jnp.broadcast_to(value[None], (len(members[0]),) + value.shape), members)


def add_up(pieces):
    return jnp.sum(pieces.astype(F32), 0).astype(BF16)


def total_grads(keep, send, core):
    plane, column = groups()
    half, width, _ = keep.shape
    mine = (keep + partner(send)).astype(BF16)
    mine = mine.reshape(len(plane[0]), half * width // len(plane[0]), width)
    mine = add_up(exchange(mine, plane))
    mine = add_up(to_all(mine, column))
    mine = to_all(mine, plane).reshape(half, width, width)
    other = partner(mine)
    first = jnp.where(core == 0, mine, other)
    second = jnp.where(core == 0, other, mine)
    return jnp.concatenate([first, second], 0).astype(F32)


def body(frames, w_query, w_key, w_value, w_out, valid_counts, out_grad):
    core = lax.axis_index("dp") % CORES
    prev_frames = shifted(frames, "seq", 1)
    prev_counts = shifted(valid_counts, "seq", 1)
    attended, own, back, keep, send = attention(
        valid_counts, prev_counts, core[None], frames, prev_frames, out_grad, w_query, w_key, w_value, w_out
    )
    returned = shifted(back, "seq", -1)
    weight_grads = total_grads(keep, send, core)
    frame_grads = (own + returned.astype(F32)).astype(BF16)
    return (attended, frame_grads, weight_grads)


def solution(mesh):
    in_specs = (P("dp", "seq", None), P(), P(), P(), P(), P("dp", "seq"), P("dp", "seq", None))
    out_specs = (P("dp", "seq", None), P("dp", "seq", None), P())
    return jax.shard_map(body, mesh=mesh, in_specs=in_specs, out_specs=out_specs, check_vma=False)
```

```python
import jax
import jax.numpy as jnp
from jax import lax
from jax.experimental import pallas as pl
from jax.experimental.pallas import tpu as pltpu
from jax.sharding import PartitionSpec as P

HEADS = 4
CH = 32
CTX = 128
LENGTH_Z = 8
CORES = 2
EVERY = ("seq", "dp")
BF16 = jnp.bfloat16
F32 = jnp.float32


def shifted(value, axis, by):
    length = lax.axis_size(axis)
    pairs = [(i, i + by) for i in range(length) if 0 <= i + by < length]
    return lax.ppermute(value, axis, pairs)


def plain(left, right):
    return jnp.dot(left, right, preferred_element_type=F32)


def rows_dot(left, right):
    return lax.dot_general(left, right, (((1,), (1,)), ((), ())), preferred_element_type=F32)


def cols_dot(left, right):
    return lax.dot_general(left, right, (((0,), (0,)), ((), ())), preferred_element_type=F32)


def projection_kernel(x_ref, g_ref, wq_ref, wk_ref, wv_ref, wo_ref, q_ref, k_ref, v_ref, dc_ref):
    batch, local, width = x_ref.shape
    x = x_ref[...].reshape(batch * local, width)
    g = g_ref[...].reshape(batch * local, width)

    def spread(value):
        return value.astype(BF16).reshape(batch, local, width)

    q_ref[...] = spread(plain(x, wq_ref[...]))
    k_ref[...] = spread(plain(x, wk_ref[...]))
    v_ref[...] = spread(plain(x, wv_ref[...]))
    dc_ref[...] = spread(rows_dot(g, wo_ref[...]))


def projections(x, g, w_query, w_key, w_value, w_out):
    vmem = pl.BlockSpec(memory_space=pltpu.VMEM)
    return pl.pallas_call(
        projection_kernel,
        out_shape=[jax.ShapeDtypeStruct(x.shape, BF16)] * 4,
        in_specs=[vmem] * 6,
        out_specs=[vmem] * 4,
        name="projections",
    )(x, g, w_query, w_key, w_value, w_out)


def attention_kernel(
    own_counts, prev_counts, core_ref, q_hbm, k_hbm, v_hbm, dc_hbm, x_hbm, xp_hbm, g_hbm, wq_hbm, wk_hbm, wv_hbm, wo_hbm,
    att_hbm, fg_hbm, fgp_hbm, keep_hbm, send_hbm,
    x_ref, xp_ref, g_ref, wq_ref, wk_ref, wv_ref, wo_ref, att_ref, fg_ref, fgp_ref, grad_ref,
    q_s, k_s, v_s, dc_s, ctx_s, dq_s, dk_s, dv_s, in_sem, out_sem,
):
    batch, local, width = x_ref.shape
    size = width // HEADS
    scale = size ** (-0.5)
    keys = CTX + local
    many = HEADS * local
    rows = batch * local
    core = core_ref[0]

    own = pl.ds(CTX, local)
    sources = [xp_hbm, wk_hbm, wv_hbm, q_hbm, k_hbm, v_hbm, dc_hbm, x_hbm, g_hbm, wo_hbm, wq_hbm]
    targets = [xp_ref, wk_ref, wv_ref, q_s, k_s.at[:, own, :], v_s.at[:, own, :], dc_s, x_ref, g_ref, wo_ref, wq_ref]
    loads = [pltpu.make_async_copy(s, t, in_sem.at[i]) for i, (s, t) in enumerate(zip(sources, targets))]
    for load in loads:
        load.start()

    def grad_store(i, first):
        out = keep_hbm if (i < 2) == first else send_hbm
        return pltpu.make_async_copy(grad_ref.at[i], out.at[i % 2], out_sem.at[i])

    def send_grad(i, value):
        grad_ref[i] = value

        @pl.when(core == 0)
        def _():
            grad_store(i, True).start()

        @pl.when(core != 0)
        def _():
            grad_store(i, False).start()

    stores = [
        pltpu.make_async_copy(fg_ref, fg_hbm, out_sem.at[4]),
        pltpu.make_async_copy(fgp_ref, fgp_hbm, out_sem.at[5]),
        pltpu.make_async_copy(att_ref, att_hbm, out_sem.at[6]),
    ]

    def spread(value):
        return value.astype(BF16).reshape(batch, local, width)

    for load in loads[:3]:
        load.wait()
    xp = xp_ref[...].reshape(rows, width)
    k_s[:, :CTX, :] = spread(plain(xp, wk_ref[...]))
    v_s[:, :CTX, :] = spread(plain(xp, wv_ref[...]))
    for load in loads[3:7]:
        load.wait()

    head_of = lax.broadcasted_iota(jnp.int32, (local, width), 1) // size
    lane_span = (lax.broadcasted_iota(jnp.int32, (CH, many), 1) % local) // CH
    slot = lax.broadcasted_iota(jnp.int32, (CH, many), 0)

    def by_head(value):
        zero = jnp.zeros_like(value)
        return jnp.concatenate([jnp.where(head_of == h, value, zero) for h in range(HEADS)], 0)

    def own_head(wide):
        out = wide[:local]
        for h in range(1, HEADS):
            out = jnp.where(head_of == h, wide[h * local : (h + 1) * local], out)
        return out

    def one(u, carry):
        k = k_s[u]
        v = v_s[u]
        qm = by_head(q_s[u])
        dcm = by_head(dc_s[u])
        scores = rows_dot(k, qm)
        parts = []
        for s in range(keys // CH):
            count = prev_counts[u, s] if s < CTX // CH else own_counts[u, s - CTX // CH]
            behind = s - lane_span
            seen = (slot < count) & (behind >= 0) & (behind <= CTX // CH)
            parts.append(jnp.where(seen, scores[s * CH : (s + 1) * CH] * scale, F32(-1e30)))
        scores = jnp.concatenate(parts, 0)
        top = jnp.max(scores, 0, keepdims=True)
        expo = jnp.exp(scores - top)
        probs = expo * (1.0 / jnp.sum(expo, 0, keepdims=True))
        probs_b = probs.astype(BF16)
        ctx_s[u] = own_head(cols_dot(probs_b, v)).astype(BF16)
        d_probs = rows_dot(v, dcm)
        delta = jnp.sum(probs * d_probs, 0, keepdims=True)
        d_scores = (probs * (d_probs - delta) * scale).astype(BF16)
        dq_s[u] = own_head(cols_dot(d_scores, k)).astype(BF16)
        dk_s[u] = plain(d_scores, qm).astype(BF16)
        dv_s[u] = plain(probs_b, dcm).astype(BF16)
        return carry

    lax.fori_loop(0, batch, one, 0, unroll=True)

    for load in loads[7:]:
        load.wait()
    x = x_ref[...].reshape(rows, width)
    g = g_ref[...].reshape(rows, width)
    ctx = ctx_s[...].reshape(rows, width)
    dq = dq_s[...].reshape(rows, width)
    dk = dk_s[:, CTX:, :].reshape(rows, width)
    dv = dv_s[:, CTX:, :].reshape(rows, width)
    dkp = dk_s[:, :CTX, :].reshape(rows, width)
    dvp = dv_s[:, :CTX, :].reshape(rows, width)

    send_grad(0, cols_dot(x, dq))
    send_grad(1, cols_dot(x, dk) + cols_dot(xp, dkp))
    send_grad(2, cols_dot(x, dv) + cols_dot(xp, dvp))
    send_grad(3, cols_dot(ctx, g))
    total = rows_dot(dq, wq_ref[...]) + rows_dot(dk, wk_ref[...]) + rows_dot(dv, wv_ref[...])
    fg_ref[...] = total.reshape(batch, local, width)
    stores[0].start()
    fgp_ref[...] = spread(rows_dot(dkp, wk_ref[...]) + rows_dot(dvp, wv_ref[...]))
    stores[1].start()
    att_ref[...] = spread(plain(ctx, wo_ref[...]))
    stores[2].start()

    @pl.when(core == 0)
    def _():
        for i in range(4):
            grad_store(i, True).wait()

    @pl.when(core != 0)
    def _():
        for i in range(4):
            grad_store(i, False).wait()

    for store in stores:
        store.wait()


def attention(own_counts, prev_counts, core, q, k, v, dc, x, xp, g, w_query, w_key, w_value, w_out):
    batch, local, width = x.shape
    smem = pl.BlockSpec(memory_space=pltpu.SMEM)
    hbm = pl.BlockSpec(memory_space=pl.ANY)
    weight = pltpu.VMEM((width, width), BF16)
    wide = pltpu.VMEM((batch, local, width), F32)
    grad = pltpu.VMEM((4, width, width), F32)
    short = pltpu.VMEM((batch, local, width), BF16)
    long = pltpu.VMEM((batch, CTX + local, width), BF16)
    return pl.pallas_call(
        attention_kernel,
        out_shape=[
            jax.ShapeDtypeStruct((batch, local, width), BF16),
            jax.ShapeDtypeStruct((batch, local, width), F32),
            jax.ShapeDtypeStruct((batch, local, width), BF16),
            jax.ShapeDtypeStruct((2, width, width), F32),
            jax.ShapeDtypeStruct((2, width, width), F32),
        ],
        in_specs=[smem] * 3 + [hbm] * 11,
        out_specs=[hbm] * 5,
        scratch_shapes=[short] * 3 + [weight] * 4 + [short, wide, short, grad]
        + [short, long, long, short, short, short, long, long]
        + [pltpu.SemaphoreType.DMA((11,)), pltpu.SemaphoreType.DMA((7,))],
        name="attention",
    )(own_counts, prev_counts, core, q, k, v, dc, x, xp, g, w_query, w_key, w_value, w_out)


def groups():
    seq, dp = lax.axis_size("seq"), lax.axis_size("dp")
    z, c = min(LENGTH_Z, seq // 2), CORES
    y, x = seq // z, dp // c

    def at(iy, iz, ix, ic):
        return (iy * z + iz) * dp + ix * c + ic

    plane = [
        [at(iy, iz, ix, ic) for iy in range(y) for ix in range(x)] for iz in range(z) for ic in range(c)
    ]
    column = [
        [at(iy, iz, ix, ic) for iz in range(z)] for iy in range(y) for ix in range(x) for ic in range(c)
    ]
    return plane, column


def partner(value):
    pairs = [(i, i ^ 1) for i in range(lax.axis_size("dp"))]
    return lax.ppermute(value, "dp", pairs)


def exchange(value, members):
    return lax.all_to_all(value, EVERY, 0, 0, axis_index_groups=members)


def to_all(value, members):
    return exchange(jnp.broadcast_to(value[None], (len(members[0]),) + value.shape), members)


def add_up(pieces):
    return jnp.sum(pieces.astype(F32), 0).astype(BF16)


def total_grads(keep, send, core):
    plane, column = groups()
    half, width, _ = keep.shape
    mine = (keep + partner(send)).astype(BF16)
    mine = mine.reshape(len(plane[0]), half * width // len(plane[0]), width)
    mine = add_up(exchange(mine, plane))
    mine = add_up(to_all(mine, column))
    mine = to_all(mine, plane).reshape(half, width, width)
    other = partner(mine)
    first = jnp.where(core == 0, mine, other)
    second = jnp.where(core == 0, other, mine)
    return jnp.concatenate([first, second], 0).astype(F32)


def body(frames, w_query, w_key, w_value, w_out, valid_counts, out_grad):
    core = lax.axis_index("dp") % CORES
    prev_frames = shifted(frames, "seq", 1)
    prev_counts = shifted(valid_counts, "seq", 1)
    local = projections(frames, out_grad, w_query, w_key, w_value, w_out)
    attended, own, back, keep, send = attention(
        valid_counts, prev_counts, core[None], *local, frames, prev_frames, out_grad, w_query, w_key, w_value, w_out
    )
    returned = shifted(back, "seq", -1)
    weight_grads = total_grads(keep, send, core)
    frame_grads = (own + returned.astype(F32)).astype(BF16)
    return (attended, frame_grads, weight_grads)


def solution(mesh):
    in_specs = (P("dp", "seq", None), P(), P(), P(), P(), P("dp", "seq"), P("dp", "seq", None))
    out_specs = (P("dp", "seq", None), P("dp", "seq", None), P())
    return jax.shard_map(body, mesh=mesh, in_specs=in_specs, out_specs=out_specs, check_vma=False)
```
